128 devices in a mesh: gx: 4 (over y), gy: 4 (over x), gz: 8 (over z, core).
Axes of the slice: x: 4, y: 4, z: 4, core: 2. Of those that a mesh axis runs over, the one named last changes fastest.
Arguments:
- token_grad: bfloat16 [131072, 320], P(('gx', 'gy', 'gz')), may hold values from -6 to 6
- token_owner: int32 [131072, 1], P(('gx', 'gy', 'gz')), may hold values from 0 to 127; in each aligned block of 1024 rows (0 to 1023, 1024 to 2047, ...) at most 16 rows name the same one
- token_row: int32 [131072], P(('gx', 'gy', 'gz')), may hold values from 0 to 4095
- table: float32 [524288, 320], P(('gx', 'gy', 'gz')), may hold values from -6 to 6
- accum: float32 [524288], P(('gx', 'gy', 'gz')), may hold values from 0.1 to 10
Outputs:
- new_table: float32 [524288, 320], P(('gx', 'gy', 'gz'))
- new_accum: float32 [524288], P(('gx', 'gy', 'gz'))
- fresh_rows: bfloat16 [131072, 320], P(('gx', 'gy', 'gz'))
The draws below stay inside these ranges and needn't reach their ends.
Inputs may be any that keep to these rules, and one draw needn't show every extreme that they name: `token_owner`: among the 1024 tokens of one device no owner is named by more than 16 tokens.
All inputs are finite; a program needn't handle non-finite values.
Results may differ from the reference program's by a relative error of at most 0.001.
Values may be sent and summed in bfloat16 or wider, within the bound.
No kernel may reach another device: no remote copies, remote signals or barrier semaphores. Data moves between devices by JAX's collectives and lax.ppermute only.
A program may use at most 64 MiB of HBM per device.

```python
import math
import jax
import jax.numpy as jnp
import numpy as np
from jax import lax

W = 320
ROWS_DEV = 4096
TOK_DEV = 1024
OWNERS = 128
CAP = 16
TOKENS = 131072
ROWS = 524288


def plant(drawn, stream_key, low, largest):
    spot = [jax.random.randint(jax.random.fold_in(stream_key, axis), (), 0, length) for axis, length in enumerate(drawn.shape)]
    main_axis = drawn.shape.index(max(drawn.shape))
    next_to = spot[:main_axis] + [(spot[main_axis] + 1) % drawn.shape[main_axis]] + spot[main_axis + 1:]
    return drawn.at[tuple(spot)].set(low).at[tuple(next_to)].set(largest)


def levels(stream_key, dims, pieces, low, largest):
    gain, own = 1.0, jax.random.fold_in(stream_key, 6)
    for axis_at, blocks in pieces:
        draws = jnp.exp(jax.random.uniform(jax.random.fold_in(own, axis_at), (blocks,), jnp.float32, low / len(pieces), largest / len(pieces)))
        gain = gain * jnp.repeat(draws, dims[axis_at] // blocks).reshape([-1 if axis == axis_at else 1 for axis in range(len(dims))])
    return gain


def rank_table(number_of, lean):
    portions = [(1 << 20) // math.isqrt(rank ** lean) + 1 for rank in range(1, number_of + 1)]
    spread = 1 + sum(portions) // (1 << 30)
    return np.cumsum(np.array([max(1, weight // spread) for weight in portions]))


def ranked_ids(key, shape, number_of, slope):
    listing = rank_table(number_of, slope)
    lot = jax.random.randint(jax.random.fold_in(key, 1), shape, 0, int(listing[number_of - 1]))
    grade = jnp.searchsorted(jnp.asarray(listing, jnp.int32), lot, side="right")
    return jax.random.permutation(jax.random.fold_in(key, 2), number_of)[grade].astype(jnp.int32)


def routed_block(stream_key, own, number, rows, amount, top, reach, skew):
    ranking = jax.random.permutation(stream_key, amount)
    crowded, usual = load_shares(amount, rows * top, reach, skew, True), load_shares(amount, rows * top, reach, skew, False)
    places = jnp.arange(amount)

    def named(lengths, turn):
        used = int((lengths > 0).sum())
        fixed = max(1, used // 4)
        moved = fixed + (places - fixed + turn * (used - fixed)) % max(1, amount - fixed)
        return jnp.zeros((amount,), jnp.int32).at[ranking[jnp.where(places < fixed, places, moved)]].set(jnp.asarray(lengths, jnp.int32))

    lengths = jnp.where(number % 4 == 0, named(crowded, number // 4), named(usual, number - number // 4 - 1))
    mixed = jax.random.permutation(jax.random.fold_in(own, 3), amount)
    giver, receiver = mixed[0:amount // 2 * 2:2], mixed[1:amount // 2 * 2:2]
    margin = jnp.minimum(lengths[giver] - 1, reach - lengths[receiver]) // 2
    margin = jnp.where((giver == ranking[0]) | (receiver == ranking[0]) | (lengths[receiver] == 0), 0, jnp.maximum(margin, 0))
    moved = jax.random.randint(jax.random.fold_in(own, 4), (amount // 2,), 0, 1 << 20) % (margin + 1)
    lengths = lengths.at[giver].add(-moved).at[receiver].add(moved)
    members = jnp.searchsorted(jnp.cumsum(lengths), jnp.arange(rows * top), side="right").astype(jnp.int32)
    listing = members.reshape(top, rows).T
    listing = listing[jax.random.permutation(jax.random.fold_in(own, 1), rows)]
    turn = jax.random.randint(jax.random.fold_in(own, 2), (rows, 1), 0, top)
    return jnp.take_along_axis(listing, (jnp.arange(top)[None, :] + turn) % top, axis=1)


def load_shares(count, total, most, lean, full):
    weights = [(1 << 20) // math.isqrt(grade ** lean) + 1 for grade in range(1, count + 1)]
    largest = most if full else min(most, max(-(-total // count), total * weights[0] // sum(weights)))
    least = 1 if total - largest >= count - 1 else 0
    given, surplus = [largest] + [least] * (count - 1), total - largest - least * (count - 1)
    while surplus > 0:
        free = [i for i in range(1, count) if given[i] < largest] or [i for i in range(1, count) if given[i] < most]
        mass, budget = sum([weights[i] for i in free]), surplus
        for i in free:
            more = min(most - given[i], max(1, budget * weights[i] // mass), surplus)
            given[i] = given[i] + more
            surplus = surplus - more
    return np.array(given)


def normal_values(key, dims, width, most, cuts=(), kind=jnp.bfloat16):
    drawn = jax.random.normal(key, dims, jnp.float32) * width
    if len(cuts) > 0:
        drawn = levels(key, dims, cuts, -0.22, 0.18) * drawn
    return jnp.clip(drawn, min=-most, max=most).astype(kind)


def setup_inputs(seed: int = 0) -> dict:
    key_of = jax.random.split(jax.random.key(seed), 6)
    token_grad = normal_values(key_of[0], (TOKENS, W), 1.0, 6.0, ((0, 128),))
    token_owner_keys = jax.random.split(jax.random.fold_in(key_of[1], 1), TOKENS // TOK_DEV)
    token_owner_turns = jax.random.permutation(jax.random.fold_in(key_of[1], 3), TOKENS // TOK_DEV)
    token_owner = jax.vmap(lambda own, number: routed_block(jax.random.fold_in(key_of[1], 2), own, number, TOK_DEV, OWNERS, 1, CAP, 2))(token_owner_keys, token_owner_turns).reshape((TOKENS, 1))
    token_row = plant(ranked_ids(key_of[2], (TOKENS,), ROWS_DEV, 2), jax.random.fold_in(key_of[2], 3), 0, ROWS_DEV - 1).astype(jnp.int32)
    table = normal_values(key_of[3], (ROWS, W), 1.0, 6.0, ((0, 128),), jnp.float32)
    accum = jnp.clip(jnp.exp(math.log(10.0) - 4.6051702 * jax.random.uniform(key_of[4], (ROWS,), jnp.float32) ** levels(key_of[4], (ROWS,), ((0, 128),), -0.2, 0.2)), 0.1, 10.0)
    return {"token_grad": token_grad, "token_owner": token_owner, "token_row": token_row, "table": table, "accum": accum}


def reference(token_grad, token_owner, token_row, table, accum):
    owners = token_owner[:, 0]
    gradients = token_grad.astype(jnp.float32)
    tables = table.reshape(OWNERS, ROWS_DEV, W)
    accums = accum.reshape(OWNERS, ROWS_DEV)

    def update(packed):
        owner_index, table_block, accum_block = packed
        is_mine = owners == owner_index
        segment_ids = jnp.where(is_mine, token_row, ROWS_DEV).astype(jnp.int32)
        summed = jax.ops.segment_sum(jnp.where(is_mine[:, None], gradients, jnp.float32(0.0)), segment_ids, num_segments=ROWS_DEV + 1)[:ROWS_DEV]
        grown = accum_block + lax.optimization_barrier(jnp.mean(summed * summed, axis=1))
        moved = table_block - 0.5 * summed / (jnp.sqrt(grown) + 1e-08)[:, None]
        return (moved, grown)
    new_tables, new_accums = lax.map(update, (jnp.arange(OWNERS, dtype=jnp.int32), tables, accums))
    new_table = new_tables.reshape(OWNERS * ROWS_DEV, W)
    new_accum = new_accums.reshape(OWNERS * ROWS_DEV)
    row_id = (owners * ROWS_DEV + token_row).astype(jnp.int32)
    fresh_rows = jnp.take(new_table, row_id, axis=0).astype(jnp.bfloat16)
    return (new_table, new_accum, fresh_rows)
```

```python
import functools

import jax
import jax.numpy as jnp
from jax import lax
from jax.experimental import pallas as pl
from jax.experimental.pallas import tpu as pltpu
from jax.sharding import PartitionSpec as P

AXES = ("gx", "gy", "gz")
RADIX = 64
ROW_LANES = 64
LIMIT = 56 << 20


def pack_kernel(owners, cap, owner_ref, row_ref, grad_ref, send_ref, target_ref, ext_ref):
    width, tokens = grad_ref.shape
    own = owner_ref[...]
    chunk = min(256, tokens)
    first = lax.broadcasted_iota(jnp.int32, (chunk, chunk), 0)
    second = lax.broadcasted_iota(jnp.int32, (chunk, chunk), 1)
    earlier = jnp.where(first < second, 1.0, 0.0).astype(jnp.bfloat16)
    ids = lax.broadcasted_iota(jnp.int32, (owners, chunk), 0)
    seen = jnp.zeros((owners, 1), jnp.float32)
    for c in range(tokens // chunk):
        part = slice(c * chunk, (c + 1) * chunk)
        named = ids == own[:, part]
        ones = jnp.where(named, 1.0, 0.0)
        before = jnp.dot(ones.astype(jnp.bfloat16), earlier, preferred_element_type=jnp.float32)
        rank = jnp.sum(jnp.where(named, before + seen, 0.0), axis=0, keepdims=True)
        seen = seen + jnp.sum(ones, axis=1, keepdims=True)
        target_ref[:, part] = own[:, part] * cap + rank.astype(jnp.int32)
    row = row_ref[...]
    high = row // RADIX
    low = row - high * RADIX
    extra = ext_ref.shape[0] - width
    place = lax.broadcasted_iota(jnp.int32, (extra, tokens), 0)
    tail = jnp.where(place == 0, high, jnp.where(place == 1, low, 0))
    ext_ref[0:width, :] = grad_ref[...]
    ext_ref[width:, :] = tail.astype(jnp.float32).astype(jnp.bfloat16)
    target = target_ref[...]
    slots = send_ref.shape[0]
    step = min(512, slots)
    for b in range(slots // step):
        slot = lax.broadcasted_iota(jnp.int32, (step, tokens), 0) + b * step
        onehot = jnp.where(slot == target, 1.0, 0.0).astype(jnp.bfloat16)
        send_ref[b * step : (b + 1) * step, :] = lax.dot_general(
            onehot, ext_ref[...], (((1,), (1,)), ((), ())), preferred_element_type=jnp.float32
        ).astype(jnp.bfloat16)


def update_kernel(
    recv_ref, accum_ref, table_hbm, new_hbm, grown_ref, answer_ref,
    turned_ref, table_ref, new_ref, rounded_ref, in_sem, out_sem,
):
    width, rows = table_ref.shape
    slots = recv_ref.shape[0]
    tile = in_tile(rows)
    tiles = rows // tile

    def fetch(j):
        part = pl.ds(pl.multiple_of(j * tile, tile), tile)
        return pltpu.make_async_copy(table_hbm.at[:, part], table_ref.at[:, part], in_sem.at[j])

    def put(j):
        part = pl.ds(pl.multiple_of(j * tile, tile), tile)
        return pltpu.make_async_copy(new_ref.at[:, part], new_hbm.at[:, part], out_sem.at[j])

    for j in range(tiles):
        fetch(j).start()
    received = recv_ref[...]
    turned_ref[...] = received.T
    lead = received[:, width : width + 2].astype(jnp.float32).astype(jnp.int32)
    row_down = lead[:, 0:1] * RADIX + lead[:, 1:2]

    def scatter(j, carry):
        part = pl.ds(pl.multiple_of(j * tile, tile), tile)
        place = lax.broadcasted_iota(jnp.int32, (slots, tile), 1) + j * tile
        onehot = jnp.where(place == row_down, 1.0, 0.0).astype(jnp.bfloat16)
        summed = jnp.dot(turned_ref[0:width, :], onehot, preferred_element_type=jnp.float32)
        grown = accum_ref[:, part] + jnp.sum(summed * summed, axis=0, keepdims=True) / width
        grown_ref[:, part] = grown
        scale = 0.5 / (jnp.sqrt(grown) + 1e-08)
        fetch(j).wait()
        moved = table_ref[:, part] - summed * scale
        new_ref[:, part] = moved
        rounded_ref[:, part] = moved.astype(jnp.bfloat16)
        put(j).start()
        return carry

    lax.fori_loop(0, tiles, scatter, 0)
    across = turned_ref[width : width + 16, :].astype(jnp.float32).astype(jnp.int32)
    row_across = across[0:1, :] * RADIX + across[1:2, :]
    step = min(512, slots)
    for b in range(slots // step):
        place = lax.broadcasted_iota(jnp.int32, (rows, step), 0)
        onehot = jnp.where(
            place == row_across[:, b * step : (b + 1) * step], 1.0, 0.0
        ).astype(jnp.bfloat16)
        picked = jnp.dot(rounded_ref[...], onehot, preferred_element_type=jnp.float32)
        picked = picked.T.reshape(step // 16, 2, 8, width)
        lower = picked[:, 0].reshape(step // 2, width)
        upper = picked[:, 1].reshape(step // 2, width)
        answer_ref[b * step // 2 : (b + 1) * step // 2, :] = jnp.concatenate(
            [lower, upper], axis=1
        ).astype(jnp.bfloat16)
    for j in range(tiles):
        put(j).wait()


def in_tile(rows):
    return min(512, rows)


def unpack_kernel(cap, back_ref, target_ref, fresh_ref):
    width, tokens = fresh_ref.shape
    half = back_ref.shape[0]
    target = target_ref[...]
    owner = target // cap
    rank = target - owner * cap
    total = None
    for side in range(2):
        spot = jnp.where(rank // 8 == side, owner * 8 + rank - 8 * side, -1)
        place = lax.broadcasted_iota(jnp.int32, (half, tokens), 0)
        onehot = jnp.where(place == spot, 1.0, 0.0).astype(jnp.bfloat16)
        values = back_ref[:, side * width : (side + 1) * width].T
        part = jnp.dot(values, onehot, preferred_element_type=jnp.float32)
        total = part if total is None else total + part
    fresh_ref[...] = total.astype(jnp.bfloat16)


VMEM = pl.BlockSpec(memory_space=pltpu.VMEM)
ANY = pl.BlockSpec(memory_space=pl.ANY)


def pack(owner, row, grad, owners, cap):
    width, tokens = grad.shape
    wide = -(-(width + 2) // 128) * 128
    return pl.pallas_call(
        functools.partial(pack_kernel, owners, cap),
        out_shape=(
            jax.ShapeDtypeStruct((owners * cap, wide), jnp.bfloat16),
            jax.ShapeDtypeStruct((1, tokens), jnp.int32),
        ),
        in_specs=[VMEM, VMEM, VMEM],
        out_specs=(VMEM, VMEM),
        scratch_shapes=[pltpu.VMEM((wide, tokens), jnp.bfloat16)],
        compiler_params=pltpu.CompilerParams(vmem_limit_bytes=LIMIT),
        name="pack",
    )(owner, row, grad)


def update(received, accum, table):
    slots, wide = received.shape
    width, rows = table.shape
    tiles = rows // in_tile(rows)
    return pl.pallas_call(
        update_kernel,
        out_shape=(
            jax.ShapeDtypeStruct((width, rows), jnp.float32),
            jax.ShapeDtypeStruct((1, rows), jnp.float32),
            jax.ShapeDtypeStruct((slots // 2, 2 * width), jnp.bfloat16),
        ),
        in_specs=[VMEM, VMEM, ANY],
        out_specs=(ANY, VMEM, VMEM),
        scratch_shapes=[
            pltpu.VMEM((wide, slots), jnp.bfloat16),
            pltpu.VMEM((width, rows), jnp.float32),
            pltpu.VMEM((width, rows), jnp.float32),
            pltpu.VMEM((width, rows), jnp.bfloat16),
            pltpu.SemaphoreType.DMA((tiles,)),
            pltpu.SemaphoreType.DMA((tiles,)),
        ],
        compiler_params=pltpu.CompilerParams(vmem_limit_bytes=LIMIT),
        name="update",
    )(received, accum, table)


def unpack(back, target, width, cap):
    tokens = target.shape[1]
    return pl.pallas_call(
        functools.partial(unpack_kernel, cap),
        out_shape=jax.ShapeDtypeStruct((width, tokens), jnp.bfloat16),
        in_specs=[VMEM, VMEM],
        out_specs=VMEM,
        compiler_params=pltpu.CompilerParams(vmem_limit_bytes=LIMIT),
        name="unpack",
    )(back, target)


def exchange(value, devices):
    blocks = value.reshape(devices, -1, value.shape[1])
    blocks = lax.all_to_all(blocks, AXES, split_axis=0, concat_axis=0, tiled=True)
    return blocks.reshape(value.shape)


def body(token_grad, token_owner, token_row, table, accum):
    devices = lax.axis_size(AXES)
    tokens, width = token_grad.shape
    cap = 2 * tokens // devices
    send, target = pack(
        token_owner.reshape(1, tokens), token_row.reshape(1, tokens), token_grad.T, devices, cap
    )
    received = exchange(send, devices)
    new_table, new_accum, answers = update(received, accum.reshape(1, -1), table.T)
    back = exchange(answers, devices)
    fresh = unpack(back, target, width, cap)
    return (new_table.T, new_accum.reshape(-1), fresh.T)


def solution(mesh):
    split = P(AXES)
    wide = P(AXES, None)
    return jax.shard_map(
        body,
        mesh=mesh,
        in_specs=(wide, wide, split, wide, split),
        out_specs=(wide, split, wide),
        check_vma=False,
    )
```

```python
import functools

import jax
import jax.numpy as jnp
from jax import lax
from jax.experimental import pallas as pl
from jax.experimental.pallas import tpu as pltpu
from jax.sharding import PartitionSpec as P

AXES = ("gx", "gy", "gz")
RADIX = 64
ROW_LANES = 64
LIMIT = 36 << 20


def pack_kernel(
    owners, cap, owner_hbm, row_hbm, grad_hbm, send_ref, target_ref,
    ext_ref, owner_ref, row_ref, sem,
):
    width, tokens = grad_hbm.shape
    owner_load = pltpu.make_async_copy(owner_hbm, owner_ref, sem.at[0])
    row_load = pltpu.make_async_copy(row_hbm, row_ref, sem.at[1])
    load = pltpu.make_async_copy(grad_hbm, ext_ref.at[0:width, :], sem.at[2])
    owner_load.start()
    row_load.start()
    load.start()
    owner_load.wait()
    row_load.wait()
    own = owner_ref[...]
    chunk = min(256, tokens)
    first = lax.broadcasted_iota(jnp.int32, (chunk, chunk), 0)
    second = lax.broadcasted_iota(jnp.int32, (chunk, chunk), 1)
    earlier = jnp.where(first < second, 1.0, 0.0).astype(jnp.bfloat16)
    ids = lax.broadcasted_iota(jnp.int32, (owners, chunk), 0)
    seen = jnp.zeros((owners, 1), jnp.float32)
    for c in range(tokens // chunk):
        part = slice(c * chunk, (c + 1) * chunk)
        named = ids == own[:, part]
        ones = jnp.where(named, 1.0, 0.0)
        before = jnp.dot(ones.astype(jnp.bfloat16), earlier, preferred_element_type=jnp.float32)
        rank = jnp.sum(jnp.where(named, before + seen, 0.0), axis=0, keepdims=True)
        seen = seen + jnp.sum(ones, axis=1, keepdims=True)
        target_ref[:, part] = own[:, part] * cap + rank.astype(jnp.int32)
    row = row_ref[...]
    high = row // RADIX
    low = row - high * RADIX
    extra = ext_ref.shape[0] - width
    place = lax.broadcasted_iota(jnp.int32, (extra, tokens), 0)
    tail = jnp.where(place == 0, high, jnp.where(place == 1, low, 0))
    ext_ref[width:, :] = tail.astype(jnp.float32).astype(jnp.bfloat16)
    load.wait()
    slots = send_ref.shape[0]
    step = min(512, slots)
    slot = lax.broadcasted_iota(jnp.int16, (step, tokens), 0)
    target = jnp.broadcast_to(target_ref[...], (16, tokens)).astype(jnp.int16)[0:1]
    one, zero = jnp.bfloat16(1), jnp.bfloat16(0)
    for b in range(slots // step):
        onehot = jnp.where(slot == target - jnp.int16(b * step), one, zero)
        send_ref[b * step : (b + 1) * step, :] = lax.dot_general(
            onehot, ext_ref[...], (((1,), (1,)), ((), ())), preferred_element_type=jnp.float32
        ).astype(jnp.bfloat16)


def update_kernel(
    recv_ref, accum_ref, table_hbm, new_hbm, grown_ref, answer_ref,
    turned_ref, table_ref, new_ref, rounded_ref, in_sem, out_sem,
):
    width, rows = table_ref.shape
    slots = recv_ref.shape[0]
    tile = in_tile(rows)
    tiles = rows // tile

    def fetch(j):
        part = pl.ds(j * tile, tile)
        return pltpu.make_async_copy(table_hbm.at[:, part], table_ref.at[:, part], in_sem.at[j])

    def put(j):
        part = pl.ds(j * tile, tile)
        return pltpu.make_async_copy(new_ref.at[:, part], new_hbm.at[:, part], out_sem.at[j])

    for j in range(tiles):
        fetch(j).start()
    received = recv_ref[...]
    turned_ref[...] = received.T
    across = turned_ref[width : width + 16, :].astype(jnp.float32).astype(jnp.int32)
    row_across = across[0:1, :] * RADIX + across[1:2, :]
    row_across = jnp.broadcast_to(row_across, (16, slots)).astype(jnp.int16)[0:1]
    one, zero = jnp.bfloat16(1), jnp.bfloat16(0)

    def summed_of(j):
        place = lax.broadcasted_iota(jnp.int16, (tile, slots), 0)
        onehot = jnp.where(place == row_across - jnp.int16(j * tile), one, zero)
        return lax.dot_general(
            turned_ref[0:width, :], onehot, (((1,), (1,)), ((), ())),
            preferred_element_type=jnp.float32,
        )

    def settle(j, summed):
        part = pl.ds(j * tile, tile)
        grown = accum_ref[:, part] + jnp.sum(summed * summed, axis=0, keepdims=True) / width
        grown_ref[:, part] = grown
        scale = 0.5 / (jnp.sqrt(grown) + 1e-08)
        moved = table_ref[:, part] - summed * scale
        new_ref[:, part] = moved
        rounded_ref[:, part] = moved.astype(jnp.bfloat16)
        put(j).start()

    ahead = summed_of(0)
    for j in range(tiles):
        fetch(j).wait()
    for j in range(tiles):
        summed = ahead
        if j + 1 < tiles:
            ahead = summed_of(j + 1)
        settle(j, summed)

    step = min(512, slots)
    below = lax.broadcasted_iota(jnp.int16, (rows, step), 0)
    for b in range(slots // step):
        onehot = jnp.where(below == row_across[:, b * step : (b + 1) * step], one, zero)
        picked = jnp.dot(rounded_ref[...], onehot, preferred_element_type=jnp.float32)
        picked = picked.T.reshape(step // 16, 2, 8, width)
        lower = picked[:, 0].reshape(step // 2, width)
        upper = picked[:, 1].reshape(step // 2, width)
        answer_ref[b * step // 2 : (b + 1) * step // 2, :] = jnp.concatenate(
            [lower, upper], axis=1
        ).astype(jnp.bfloat16)
    for j in range(tiles):
        put(j).wait()


def in_tile(rows):
    return min(1024, rows)


def unpack_kernel(cap, back_ref, target_ref, fresh_ref):
    width, tokens = fresh_ref.shape
    half = back_ref.shape[0]
    target = target_ref[...]
    owner = target // cap
    rank = target - owner * cap
    total = None
    for side in range(2):
        spot = jnp.where(rank // 8 == side, owner * 8 + rank - 8 * side, -1)
        spot = jnp.broadcast_to(spot, (16, tokens)).astype(jnp.int16)[0:1]
        place = lax.broadcasted_iota(jnp.int16, (half, tokens), 0)
        onehot = jnp.where(place == spot, jnp.bfloat16(1), jnp.bfloat16(0))
        values = back_ref[:, side * width : (side + 1) * width].T
        part = jnp.dot(values, onehot, preferred_element_type=jnp.float32)
        total = part if total is None else total + part
    fresh_ref[...] = total.astype(jnp.bfloat16)


VMEM = pl.BlockSpec(memory_space=pltpu.VMEM)
HBM = pl.BlockSpec(memory_space=pltpu.HBM)


def pack(owner, row, grad, owners, cap):
    width, tokens = grad.shape
    wide = -(-(width + 2) // 128) * 128
    return pl.pallas_call(
        functools.partial(pack_kernel, owners, cap),
        out_shape=(
            jax.ShapeDtypeStruct((owners * cap, wide), jnp.bfloat16),
            jax.ShapeDtypeStruct((1, tokens), jnp.int32),
        ),
        in_specs=[HBM, HBM, HBM],
        out_specs=(VMEM, VMEM),
        scratch_shapes=[
            pltpu.VMEM((wide, tokens), jnp.bfloat16),
            pltpu.VMEM((1, tokens), jnp.int32),
            pltpu.VMEM((1, tokens), jnp.int32),
            pltpu.SemaphoreType.DMA((3,)),
        ],
        compiler_params=pltpu.CompilerParams(vmem_limit_bytes=LIMIT),
        name="pack",
    )(*(pltpu.with_memory_space_constraint(x, pltpu.HBM) for x in (owner, row, grad)))


def update(received, accum, table):
    slots, wide = received.shape
    width, rows = table.shape
    tiles = rows // in_tile(rows)
    return pl.pallas_call(
        update_kernel,
        out_shape=(
            jax.ShapeDtypeStruct((width, rows), jnp.float32),
            jax.ShapeDtypeStruct((1, rows), jnp.float32),
            jax.ShapeDtypeStruct((slots // 2, 2 * width), jnp.bfloat16),
        ),
        in_specs=[VMEM, VMEM, HBM],
        out_specs=(HBM, VMEM, VMEM),
        scratch_shapes=[
            pltpu.VMEM((wide, slots), jnp.bfloat16),
            pltpu.VMEM((width, rows), jnp.float32),
            pltpu.VMEM((width, rows), jnp.float32),
            pltpu.VMEM((width, rows), jnp.bfloat16),
            pltpu.SemaphoreType.DMA((tiles,)),
            pltpu.SemaphoreType.DMA((tiles,)),
        ],
        compiler_params=pltpu.CompilerParams(vmem_limit_bytes=LIMIT),
        name="update",
    )(received, accum, pltpu.with_memory_space_constraint(table, pltpu.HBM))


def unpack(back, target, width, cap):
    tokens = target.shape[1]
    return pl.pallas_call(
        functools.partial(unpack_kernel, cap),
        out_shape=jax.ShapeDtypeStruct((width, tokens), jnp.bfloat16),
        in_specs=[VMEM, VMEM],
        out_specs=VMEM,
        compiler_params=pltpu.CompilerParams(vmem_limit_bytes=LIMIT),
        name="unpack",
    )(back, target)


def exchange(value, devices):
    blocks = value.reshape(devices, -1, value.shape[1])
    blocks = lax.all_to_all(blocks, AXES, split_axis=0, concat_axis=0, tiled=True)
    return blocks.reshape(value.shape)


def body(token_grad, token_owner, token_row, table, accum):
    devices = lax.axis_size(AXES)
    tokens, width = token_grad.shape
    cap = 2 * tokens // devices
    send, target = pack(
        token_owner.reshape(1, tokens), token_row.reshape(1, tokens), token_grad.T, devices, cap
    )
    received = exchange(send, devices)
    new_table, new_accum, answers = update(received, accum.reshape(1, -1), table.T)
    back = exchange(answers, devices)
    fresh = unpack(back, target, width, cap)
    return (new_table.T, new_accum.reshape(-1), fresh.T)


def solution(mesh):
    split = P(AXES)
    wide = P(AXES, None)
    return jax.shard_map(
        body,
        mesh=mesh,
        in_specs=(wide, wide, split, wide, split),
        out_specs=(wide, split, wide),
        check_vma=False,
    )
```

```python
import functools

import jax
import jax.numpy as jnp
from jax import lax
from jax.experimental import pallas as pl
from jax.experimental.pallas import tpu as pltpu
from jax.sharding import PartitionSpec as P

AXES = ("gx", "gy", "gz")
RADIX = 64
ROW_LANES = 64
LIMIT = 36 << 20


def pack_kernel(
    owners, cap, owner_hbm, row_hbm, grad_hbm, send_ref, target_ref,
    ext_ref, owner_ref, row_ref, sem,
):
    width, tokens = grad_hbm.shape
    owner_load = pltpu.make_async_copy(owner_hbm, owner_ref, sem.at[0])
    row_load = pltpu.make_async_copy(row_hbm, row_ref, sem.at[1])
    load = pltpu.make_async_copy(grad_hbm, ext_ref.at[0:width, :], sem.at[2])
    owner_load.start()
    row_load.start()
    load.start()
    owner_load.wait()
    row_load.wait()
    own = owner_ref[...]
    chunk = min(256, tokens)
    first = lax.broadcasted_iota(jnp.int32, (chunk, chunk), 0)
    second = lax.broadcasted_iota(jnp.int32, (chunk, chunk), 1)
    earlier = jnp.where(first < second, 1.0, 0.0).astype(jnp.bfloat16)
    ids = lax.broadcasted_iota(jnp.int32, (owners, chunk), 0)
    seen = jnp.zeros((owners, 1), jnp.float32)
    for c in range(tokens // chunk):
        part = slice(c * chunk, (c + 1) * chunk)
        named = ids == own[:, part]
        ones = jnp.where(named, 1.0, 0.0)
        before = jnp.dot(ones.astype(jnp.bfloat16), earlier, preferred_element_type=jnp.float32)
        rank = jnp.sum(jnp.where(named, before + seen, 0.0), axis=0, keepdims=True)
        seen = seen + jnp.sum(ones, axis=1, keepdims=True)
        target_ref[:, part] = own[:, part] * cap + rank.astype(jnp.int32)
    row = row_ref[...]
    high = row // RADIX
    low = row - high * RADIX
    extra = ext_ref.shape[0] - width
    place = lax.broadcasted_iota(jnp.int32, (extra, tokens), 0)
    tail = jnp.where(place == 0, high, jnp.where(place == 1, low, 0))
    ext_ref[width:, :] = tail.astype(jnp.float32).astype(jnp.bfloat16)
    load.wait()
    slots = send_ref.shape[0]
    wide = width + 16
    step = min(512, slots)
    slot = lax.broadcasted_iota(jnp.int16, (step, tokens), 0)
    target = jnp.broadcast_to(target_ref[...], (16, tokens)).astype(jnp.int16)[0:1]
    one, zero = jnp.bfloat16(1), jnp.bfloat16(0)
    for b in range(slots // step):
        onehot = jnp.where(slot == target - jnp.int16(b * step), one, zero)
        placed = lax.dot_general(
            ext_ref[0:wide, :], onehot, (((1,), (1,)), ((), ())),
            preferred_element_type=jnp.float32,
        ).astype(jnp.bfloat16)
        send_ref[b * step : (b + 1) * step, 0:wide] = placed.T


def update_kernel(
    recv_ref, accum_ref, table_hbm, new_hbm, grown_ref, answer_ref,
    turned_ref, table_ref, new_ref, rounded_ref, in_sem, out_sem,
):
    width, rows = table_ref.shape
    slots = recv_ref.shape[0]
    tile = in_tile(rows)
    tiles = rows // tile

    def fetch(j):
        part = pl.ds(j * tile, tile)
        return pltpu.make_async_copy(table_hbm.at[:, part], table_ref.at[:, part], in_sem.at[j])

    def put(j):
        part = pl.ds(j * tile, tile)
        return pltpu.make_async_copy(new_ref.at[:, part], new_hbm.at[:, part], out_sem.at[j])

    for j in range(tiles):
        fetch(j).start()
    received = recv_ref[...]
    turned_ref[...] = received.T
    across = turned_ref[width : width + 16, :].astype(jnp.float32).astype(jnp.int32)
    row_across = across[0:1, :] * RADIX + across[1:2, :]
    row_across = jnp.broadcast_to(row_across, (16, slots)).astype(jnp.int16)[0:1]
    one, zero = jnp.bfloat16(1), jnp.bfloat16(0)

    def summed_of(j):
        place = lax.broadcasted_iota(jnp.int16, (tile, slots), 0)
        onehot = jnp.where(place == row_across - jnp.int16(j * tile), one, zero)
        return lax.dot_general(
            turned_ref[0:width, :], onehot, (((1,), (1,)), ((), ())),
            preferred_element_type=jnp.float32,
        )

    def settle(j, summed):
        part = pl.ds(j * tile, tile)
        grown = accum_ref[:, part] + jnp.sum(summed * summed, axis=0, keepdims=True) / width
        grown_ref[:, part] = grown
        scale = 0.5 / (jnp.sqrt(grown) + 1e-08)
        moved = table_ref[:, part] - summed * scale
        new_ref[:, part] = moved
        rounded_ref[:, part] = moved.astype(jnp.bfloat16)

    ahead = summed_of(0)
    for j in range(tiles):
        summed = ahead
        if j + 1 < tiles:
            ahead = summed_of(j + 1)
        if j == 0:
            for i in range(tiles):
                fetch(i).wait()
        settle(j, summed)
    for j in range(tiles):
        put(j).start()

    step = min(512, slots)
    below = lax.broadcasted_iota(jnp.int16, (rows, step), 0)
    for b in range(slots // step):
        onehot = jnp.where(below == row_across[:, b * step : (b + 1) * step], one, zero)
        picked = jnp.dot(rounded_ref[...], onehot, preferred_element_type=jnp.float32)
        picked = picked.T.reshape(step // 16, 2, 8, width)
        lower = picked[:, 0].reshape(step // 2, width)
        upper = picked[:, 1].reshape(step // 2, width)
        answer_ref[b * step // 2 : (b + 1) * step // 2, :] = jnp.concatenate(
            [lower, upper], axis=1
        ).astype(jnp.bfloat16)
    for j in range(tiles):
        put(j).wait()


def in_tile(rows):
    return min(2048, rows)


def unpack_kernel(cap, back_ref, target_ref, fresh_hbm, turned_ref, fresh_ref, sem):
    width, tokens = fresh_hbm.shape
    half = back_ref.shape[0]
    target = target_ref[...]
    owner = target // cap
    rank = target - owner * cap
    side = rank // 8
    spot = side * half + owner * 8 + rank - 8 * side
    spot = jnp.broadcast_to(spot, (16, tokens)).astype(jnp.int16)[0:1]
    turned = back_ref[...].T
    turned_ref[:, 0:half] = turned[0:width]
    turned_ref[:, half:] = turned[width:]
    step = tokens // 2
    place = lax.broadcasted_iota(jnp.int16, (2 * half, step), 0)
    copies = []
    for b in range(2):
        part = slice(b * step, (b + 1) * step)
        onehot = jnp.where(place == spot[:, part], jnp.bfloat16(1), jnp.bfloat16(0))
        fresh_ref[:, part] = jnp.dot(
            turned_ref[...], onehot, preferred_element_type=jnp.float32
        ).astype(jnp.bfloat16)
        copy = pltpu.make_async_copy(fresh_ref.at[:, part], fresh_hbm.at[:, part], sem.at[b])
        copy.start()
        copies.append(copy)
    for copy in copies:
        copy.wait()


VMEM = pl.BlockSpec(memory_space=pltpu.VMEM)
HBM = pl.BlockSpec(memory_space=pltpu.HBM)


def pack(owner, row, grad, owners, cap):
    width, tokens = grad.shape
    wide = -(-(width + 2) // 128) * 128
    return pl.pallas_call(
        functools.partial(pack_kernel, owners, cap),
        out_shape=(
            jax.ShapeDtypeStruct((owners * cap, wide), jnp.bfloat16),
            jax.ShapeDtypeStruct((1, tokens), jnp.int32),
        ),
        in_specs=[HBM, HBM, HBM],
        out_specs=(VMEM, VMEM),
        scratch_shapes=[
            pltpu.VMEM((wide, tokens), jnp.bfloat16),
            pltpu.VMEM((1, tokens), jnp.int32),
            pltpu.VMEM((1, tokens), jnp.int32),
            pltpu.SemaphoreType.DMA((3,)),
        ],
        compiler_params=pltpu.CompilerParams(vmem_limit_bytes=LIMIT),
        name="pack",
    )(*(pltpu.with_memory_space_constraint(x, pltpu.HBM) for x in (owner, row, grad)))


def update(received, accum, table):
    slots, wide = received.shape
    width, rows = table.shape
    tiles = rows // in_tile(rows)
    return pl.pallas_call(
        update_kernel,
        out_shape=(
            jax.ShapeDtypeStruct((width, rows), jnp.float32),
            jax.ShapeDtypeStruct((1, rows), jnp.float32),
            jax.ShapeDtypeStruct((slots // 2, 2 * width), jnp.bfloat16),
        ),
        in_specs=[VMEM, VMEM, HBM],
        out_specs=(HBM, VMEM, VMEM),
        scratch_shapes=[
            pltpu.VMEM((wide, slots), jnp.bfloat16),
            pltpu.VMEM((width, rows), jnp.float32),
            pltpu.VMEM((width, rows), jnp.float32),
            pltpu.VMEM((width, rows), jnp.bfloat16),
            pltpu.SemaphoreType.DMA((tiles,)),
            pltpu.SemaphoreType.DMA((tiles,)),
        ],
        compiler_params=pltpu.CompilerParams(vmem_limit_bytes=LIMIT),
        name="update",
    )(received, accum, pltpu.with_memory_space_constraint(table, pltpu.HBM))


def unpack(back, target, width, cap):
    tokens = target.shape[1]
    return pl.pallas_call(
        functools.partial(unpack_kernel, cap),
        out_shape=jax.ShapeDtypeStruct((width, tokens), jnp.bfloat16),
        in_specs=[VMEM, VMEM],
        out_specs=HBM,
        scratch_shapes=[
            pltpu.VMEM((width, 2 * back.shape[0]), jnp.bfloat16),
            pltpu.VMEM((width, tokens), jnp.bfloat16),
            pltpu.SemaphoreType.DMA((2,)),
        ],
        compiler_params=pltpu.CompilerParams(vmem_limit_bytes=LIMIT),
        name="unpack",
    )(back, target)


def exchange(value, devices):
    blocks = value.reshape(devices, -1, value.shape[1])
    blocks = lax.all_to_all(blocks, AXES, split_axis=0, concat_axis=0, tiled=True)
    return blocks.reshape(value.shape)


def body(token_grad, token_owner, token_row, table, accum):
    devices = lax.axis_size(AXES)
    tokens, width = token_grad.shape
    cap = 2 * tokens // devices
    send, target = pack(
        token_owner.reshape(1, tokens), token_row.reshape(1, tokens), token_grad.T, devices, cap
    )
    received = exchange(send, devices)
    new_table, new_accum, answers = update(received, accum.reshape(1, -1), table.T)
    back = exchange(answers, devices)
    fresh = unpack(back, target, width, cap)
    return (new_table.T, new_accum.reshape(-1), fresh.T)


def solution(mesh):
    split = P(AXES)
    wide = P(AXES, None)
    return jax.shard_map(
        body,
        mesh=mesh,
        in_specs=(wide, wide, split, wide, split),
        out_specs=(wide, split, wide),
        check_vma=False,
    )
```

```python
import functools

import jax
import jax.numpy as jnp
from jax import lax
from jax.experimental import pallas as pl
from jax.experimental.pallas import tpu as pltpu
from jax.sharding import PartitionSpec as P

AXES = ("gx", "gy", "gz")
RADIX = 64
ROW_LANES = 64
LIMIT = 36 << 20


def pack_kernel(
    owners, cap, owner_hbm, row_hbm, grad_hbm, send_ref, target_ref,
    ext_ref, owner_ref, row_ref, sem,
):
    width, tokens = grad_hbm.shape
    owner_load = pltpu.make_async_copy(owner_hbm, owner_ref, sem.at[0])
    row_load = pltpu.make_async_copy(row_hbm, row_ref, sem.at[1])
    load = pltpu.make_async_copy(grad_hbm, ext_ref.at[0:width, :], sem.at[2])
    owner_load.start()
    row_load.start()
    load.start()
    owner_load.wait()
    row_load.wait()
    own = owner_ref[...]
    chunk = min(256, tokens)
    first = lax.broadcasted_iota(jnp.int32, (chunk, chunk), 0)
    second = lax.broadcasted_iota(jnp.int32, (chunk, chunk), 1)
    earlier = jnp.where(first < second, 1.0, 0.0).astype(jnp.bfloat16)
    ids = lax.broadcasted_iota(jnp.int32, (owners, chunk), 0)
    seen = jnp.zeros((owners, 1), jnp.float32)
    for c in range(tokens // chunk):
        part = slice(c * chunk, (c + 1) * chunk)
        named = ids == own[:, part]
        ones = jnp.where(named, 1.0, 0.0)
        before = jnp.dot(ones.astype(jnp.bfloat16), earlier, preferred_element_type=jnp.float32)
        rank = jnp.sum(jnp.where(named, before + seen, 0.0), axis=0, keepdims=True)
        seen = seen + jnp.sum(ones, axis=1, keepdims=True)
        target_ref[:, part] = own[:, part] * cap + rank.astype(jnp.int32)
    row = row_ref[...]
    high = row // RADIX
    low = row - high * RADIX
    extra = ext_ref.shape[0] - width
    place = lax.broadcasted_iota(jnp.int32, (extra, tokens), 0)
    tail = jnp.where(place == 0, high, jnp.where(place == 1, low, 0))
    ext_ref[width:, :] = tail.astype(jnp.float32).astype(jnp.bfloat16)
    load.wait()
    slots = send_ref.shape[0]
    wide = width + 16
    step = min(512, slots)
    slot = lax.broadcasted_iota(jnp.int16, (step, tokens), 0)
    target = jnp.broadcast_to(target_ref[...], (16, tokens)).astype(jnp.int16)[0:1]
    one, zero = jnp.bfloat16(1), jnp.bfloat16(0)
    for b in range(slots // step):
        onehot = jnp.where(slot == target - jnp.int16(b * step), one, zero)
        placed = lax.dot_general(
            ext_ref[0:wide, :], onehot, (((1,), (1,)), ((), ())),
            preferred_element_type=jnp.float32,
        ).astype(jnp.bfloat16)
        send_ref[b * step : (b + 1) * step, 0:wide] = placed.T


def copies_of(source, target, sem):
    count = sem.shape[0]
    piece = source.shape[1] // count
    parts = [slice(i * piece, (i + 1) * piece) for i in range(count)]
    return [
        pltpu.make_async_copy(source.at[:, part], target.at[:, part], sem.at[i])
        for i, part in enumerate(parts)
    ]


def update_kernel(
    recv_ref, accum_ref, table_ref, new_ref, grown_ref, answer_ref, turned_ref, rounded_ref
):
    width, rows = table_ref.shape
    slots = recv_ref.shape[0]
    tile = in_tile(rows)
    tiles = rows // tile
    turned_ref[...] = recv_ref[...].T
    across = turned_ref[width : width + 16, :].astype(jnp.float32).astype(jnp.int32)
    row_across = across[0:1, :] * RADIX + across[1:2, :]
    row_across = jnp.broadcast_to(row_across, (16, slots)).astype(jnp.int16)[0:1]
    one, zero = jnp.bfloat16(1), jnp.bfloat16(0)

    def summed_of(j):
        place = lax.broadcasted_iota(jnp.int16, (tile, slots), 0)
        onehot = jnp.where(place == row_across - jnp.int16(j * tile), one, zero)
        return lax.dot_general(
            turned_ref[0:width, :], onehot, (((1,), (1,)), ((), ())),
            preferred_element_type=jnp.float32,
        )

    def settle(j, summed):
        part = pl.ds(j * tile, tile)
        grown = accum_ref[:, part] + jnp.sum(summed * summed, axis=0, keepdims=True) / width
        grown_ref[:, part] = grown
        scale = 0.5 / (jnp.sqrt(grown) + 1e-08)
        moved = table_ref[:, part] - summed * scale
        new_ref[:, part] = moved
        rounded_ref[:, part] = moved.astype(jnp.bfloat16)

    ahead = summed_of(0)
    for j in range(tiles):
        summed = ahead
        if j + 1 < tiles:
            ahead = summed_of(j + 1)
        settle(j, summed)

    step = min(512, slots)
    below = lax.broadcasted_iota(jnp.int16, (rows, step), 0)
    for b in range(slots // step):
        onehot = jnp.where(below == row_across[:, b * step : (b + 1) * step], one, zero)
        picked = jnp.dot(rounded_ref[...], onehot, preferred_element_type=jnp.float32)
        picked = picked.T.reshape(step // 16, 2, 8, width)
        lower = picked[:, 0].reshape(step // 2, width)
        upper = picked[:, 1].reshape(step // 2, width)
        answer_ref[b * step // 2 : (b + 1) * step // 2, :] = jnp.concatenate(
            [lower, upper], axis=1
        ).astype(jnp.bfloat16)


def in_tile(rows):
    return min(2048, rows)


def unpack_kernel(
    cap, back_ref, target_ref, table_ref, fresh_hbm, table_hbm, turned_ref, fresh_ref, sem, table_sem
):
    copies = copies_of(table_ref, table_hbm, table_sem)
    for copy in copies:
        copy.start()
    width, tokens = fresh_hbm.shape
    half = back_ref.shape[0]
    target = target_ref[...]
    owner = target // cap
    rank = target - owner * cap
    side = rank // 8
    spot = side * half + owner * 8 + rank - 8 * side
    spot = jnp.broadcast_to(spot, (16, tokens)).astype(jnp.int16)[0:1]
    turned = back_ref[...].T
    turned_ref[:, 0:half] = turned[0:width]
    turned_ref[:, half:] = turned[width:]
    step = tokens // 2
    place = lax.broadcasted_iota(jnp.int16, (2 * half, step), 0)
    for b in range(2):
        part = slice(b * step, (b + 1) * step)
        onehot = jnp.where(place == spot[:, part], jnp.bfloat16(1), jnp.bfloat16(0))
        fresh_ref[:, part] = jnp.dot(
            turned_ref[...], onehot, preferred_element_type=jnp.float32
        ).astype(jnp.bfloat16)
        copy = pltpu.make_async_copy(fresh_ref.at[:, part], fresh_hbm.at[:, part], sem.at[b])
        copy.start()
        copies.append(copy)
    for copy in copies:
        copy.wait()


def cost(depth, rows, columns, *arrays):
    moved = sum(x.size * x.dtype.itemsize for x in arrays)
    return pl.CostEstimate(
        flops=2 * depth * rows * columns, transcendentals=0, bytes_accessed=moved
    )


VMEM = pl.BlockSpec(memory_space=pltpu.VMEM)
HBM = pl.BlockSpec(memory_space=pltpu.HBM)


def pack(owner, row, grad, owners, cap):
    width, tokens = grad.shape
    wide = -(-(width + 2) // 128) * 128
    sent = jax.ShapeDtypeStruct((owners * cap, wide), jnp.bfloat16)
    return pl.pallas_call(
        functools.partial(pack_kernel, owners, cap),
        out_shape=(
            sent,
            jax.ShapeDtypeStruct((1, tokens), jnp.int32),
        ),
        in_specs=[HBM, HBM, HBM],
        out_specs=(VMEM, VMEM),
        scratch_shapes=[
            pltpu.VMEM((wide, tokens), jnp.bfloat16),
            pltpu.VMEM((1, tokens), jnp.int32),
            pltpu.VMEM((1, tokens), jnp.int32),
            pltpu.SemaphoreType.DMA((3,)),
        ],
        compiler_params=pltpu.CompilerParams(vmem_limit_bytes=LIMIT),
        cost_estimate=cost(tokens, owners * cap, wide, owner, row, grad, sent),
        name="pack",
    )(*(pltpu.with_memory_space_constraint(x, pltpu.HBM) for x in (owner, row, grad)))


def update(received, accum, table):
    slots, wide = received.shape
    width, rows = table.shape
    return pl.pallas_call(
        update_kernel,
        out_shape=(
            jax.ShapeDtypeStruct((width, rows), jnp.float32),
            jax.ShapeDtypeStruct((1, rows), jnp.float32),
            jax.ShapeDtypeStruct((slots // 2, 2 * width), jnp.bfloat16),
        ),
        in_specs=[VMEM, VMEM, VMEM],
        out_specs=(VMEM, VMEM, VMEM),
        scratch_shapes=[
            pltpu.VMEM((wide, slots), jnp.bfloat16),
            pltpu.VMEM((width, rows), jnp.bfloat16),
        ],
        compiler_params=pltpu.CompilerParams(vmem_limit_bytes=LIMIT),
        cost_estimate=cost(2 * slots, rows, width, received, accum, table, table),
        name="update",
    )(received, accum, table)


def unpack(back, target, table, cap):
    tokens = target.shape[1]
    width = table.shape[0]
    return pl.pallas_call(
        functools.partial(unpack_kernel, cap),
        out_shape=(
            jax.ShapeDtypeStruct((width, tokens), jnp.bfloat16),
            jax.ShapeDtypeStruct(table.shape, jnp.float32),
        ),
        in_specs=[VMEM, VMEM, VMEM],
        out_specs=(HBM, HBM),
        scratch_shapes=[
            pltpu.VMEM((width, 2 * back.shape[0]), jnp.bfloat16),
            pltpu.VMEM((width, tokens), jnp.bfloat16),
            pltpu.SemaphoreType.DMA((2,)),
            pltpu.SemaphoreType.DMA((4,)),
        ],
        compiler_params=pltpu.CompilerParams(vmem_limit_bytes=LIMIT),
        cost_estimate=cost(2 * back.shape[0], width, tokens, back, table),
        name="unpack",
    )(back, target, table)


def exchange(value, devices):
    blocks = value.reshape(devices, -1, value.shape[1])
    blocks = lax.all_to_all(blocks, AXES, split_axis=0, concat_axis=0, tiled=True)
    return blocks.reshape(value.shape)


def body(token_grad, token_owner, token_row, table, accum):
    devices = lax.axis_size(AXES)
    tokens, width = token_grad.shape
    cap = 2 * tokens // devices
    send, target = pack(
        token_owner.reshape(1, tokens), token_row.reshape(1, tokens), token_grad.T, devices, cap
    )
    received = exchange(send, devices)
    updated, new_accum, answers = update(received, accum.reshape(1, -1), table.T)
    back = exchange(answers, devices)
    fresh, new_table = unpack(back, target, updated, cap)
    return (new_table.T, new_accum.reshape(-1), fresh.T)


def solution(mesh):
    split = P(AXES)
    wide = P(AXES, None)
    return jax.shard_map(
        body,
        mesh=mesh,
        in_specs=(wide, wide, split, wide, split),
        out_specs=(wide, split, wide),
        check_vma=False,
    )
```

```python
import functools

import jax
import jax.numpy as jnp
from jax import lax
from jax.experimental import pallas as pl
from jax.experimental.pallas import tpu as pltpu
from jax.sharding import PartitionSpec as P

AXES = ("gx", "gy", "gz")
RADIX = 64
ROW_LANES = 64
LIMIT = 36 << 20


def pack_kernel(
    owners, cap, owner_hbm, row_hbm, grad_hbm, send_ref, target_ref,
    ext_ref, owner_ref, row_ref, sem,
):
    width, tokens = grad_hbm.shape
    owner_load = pltpu.make_async_copy(owner_hbm, owner_ref, sem.at[0])
    row_load = pltpu.make_async_copy(row_hbm, row_ref, sem.at[1])
    load = pltpu.make_async_copy(grad_hbm, ext_ref.at[0:width, :], sem.at[2])
    owner_load.start()
    row_load.start()
    load.start()
    owner_load.wait()
    row_load.wait()
    own = owner_ref[...]
    chunk = min(256, tokens)
    first = lax.broadcasted_iota(jnp.int32, (chunk, chunk), 0)
    second = lax.broadcasted_iota(jnp.int32, (chunk, chunk), 1)
    earlier = jnp.where(first < second, 1.0, 0.0).astype(jnp.bfloat16)
    ids = lax.broadcasted_iota(jnp.int32, (owners, chunk), 0)
    seen = jnp.zeros((owners, 1), jnp.float32)
    for c in range(tokens // chunk):
        part = slice(c * chunk, (c + 1) * chunk)
        named = ids == own[:, part]
        ones = jnp.where(named, 1.0, 0.0)
        before = jnp.dot(ones.astype(jnp.bfloat16), earlier, preferred_element_type=jnp.float32)
        rank = jnp.sum(jnp.where(named, before + seen, 0.0), axis=0, keepdims=True)
        seen = seen + jnp.sum(ones, axis=1, keepdims=True)
        target_ref[:, part] = own[:, part] * cap + rank.astype(jnp.int32)
    row = row_ref[...]
    high = row // RADIX
    low = row - high * RADIX
    extra = ext_ref.shape[0] - width
    place = lax.broadcasted_iota(jnp.int32, (extra, tokens), 0)
    tail = jnp.where(place == 0, high, jnp.where(place == 1, low, 0))
    ext_ref[width:, :] = tail.astype(jnp.float32).astype(jnp.bfloat16)
    load.wait()
    slots = send_ref.shape[0]
    wide = width + 16
    step = min(512, slots)
    slot = lax.broadcasted_iota(jnp.int16, (step, tokens), 0)
    target = jnp.broadcast_to(target_ref[...], (16, tokens)).astype(jnp.int16)[0:1]
    one, zero = jnp.bfloat16(1), jnp.bfloat16(0)
    for b in range(slots // step):
        onehot = jnp.where(slot == target - jnp.int16(b * step), one, zero)
        placed = lax.dot_general(
            ext_ref[0:wide, :], onehot, (((1,), (1,)), ((), ())),
            preferred_element_type=jnp.float32,
        ).astype(jnp.bfloat16)
        send_ref[b * step : (b + 1) * step, 0:wide] = placed.T


def copies_of(source, target, sem):
    count = sem.shape[0]
    piece = source.shape[1] // count
    parts = [slice(i * piece, (i + 1) * piece) for i in range(count)]
    return [
        pltpu.make_async_copy(source.at[:, part], target.at[:, part], sem.at[i])
        for i, part in enumerate(parts)
    ]


def update_kernel(
    recv_ref, accum_ref, table_ref, new_hbm, rest_ref, grown_hbm, answer_ref,
    turned_ref, rounded_ref, grown_ref, sem, new_ref, new_sem,
):
    width, rows = table_ref.shape
    slots = recv_ref.shape[0]
    tile = in_tile(rows)
    tiles = rows // tile
    turned_ref[...] = recv_ref[...].T
    across = turned_ref[width : width + 16, :].astype(jnp.float32).astype(jnp.int32)
    row_across = across[0:1, :] * RADIX + across[1:2, :]
    row_across = jnp.broadcast_to(row_across, (16, slots)).astype(jnp.int16)[0:1]
    one, zero = jnp.bfloat16(1), jnp.bfloat16(0)

    def summed_of(j):
        place = lax.broadcasted_iota(jnp.int16, (tile, slots), 0)
        onehot = jnp.where(place == row_across - jnp.int16(j * tile), one, zero)
        return lax.dot_general(
            turned_ref[0:width, :], onehot, (((1,), (1,)), ((), ())),
            preferred_element_type=jnp.float32,
        )

    def settle(j, summed):
        part = pl.ds(j * tile, tile)
        grown = accum_ref[:, part] + jnp.sum(summed * summed, axis=0, keepdims=True) / width
        grown_ref[:, part] = grown
        scale = 0.5 / (jnp.sqrt(grown) + 1e-08)
        moved = table_ref[:, part] - summed * scale
        if j + 1 < tiles:
            new_ref[:, part] = moved
        else:
            rest_ref[...] = moved
        rounded_ref[:, part] = moved.astype(jnp.bfloat16)

    ahead = summed_of(0)
    for j in range(tiles):
        summed = ahead
        if j + 1 < tiles:
            ahead = summed_of(j + 1)
        settle(j, summed)
    grown_copy = pltpu.make_async_copy(grown_ref, grown_hbm, sem)
    grown_copy.start()
    early = rows - tile
    copies = copies_of(new_ref, new_hbm.at[:, 0:early], new_sem)
    for copy in copies:
        copy.start()

    step = min(512, slots)
    below = lax.broadcasted_iota(jnp.int16, (rows, step), 0)
    for b in range(slots // step):
        onehot = jnp.where(below == row_across[:, b * step : (b + 1) * step], one, zero)
        picked = jnp.dot(rounded_ref[...], onehot, preferred_element_type=jnp.float32)
        picked = picked.T.reshape(step // 16, 2, 8, width)
        lower = picked[:, 0].reshape(step // 2, width)
        upper = picked[:, 1].reshape(step // 2, width)
        answer_ref[b * step // 2 : (b + 1) * step // 2, :] = jnp.concatenate(
            [lower, upper], axis=1
        ).astype(jnp.bfloat16)
    grown_copy.wait()
    for copy in copies:
        copy.wait()


def in_tile(rows):
    return min(2048, rows)


def unpack_kernel(
    cap, back_ref, target_ref, rest_ref, part_hbm, fresh_hbm, table_hbm, turned_ref, fresh_ref, sem, table_sem
):
    rows, tile = table_hbm.shape[1], rest_ref.shape[1]
    copies = copies_of(rest_ref, table_hbm.at[:, rows - tile : rows], table_sem)
    for copy in copies:
        copy.start()
    width, tokens = fresh_hbm.shape
    half = back_ref.shape[0]
    target = target_ref[...]
    owner = target // cap
    rank = target - owner * cap
    side = rank // 8
    spot = side * half + owner * 8 + rank - 8 * side
    spot = jnp.broadcast_to(spot, (16, tokens)).astype(jnp.int16)[0:1]
    turned = back_ref[...].T
    turned_ref[:, 0:half] = turned[0:width]
    turned_ref[:, half:] = turned[width:]
    step = tokens // 2
    place = lax.broadcasted_iota(jnp.int16, (2 * half, step), 0)
    for b in range(2):
        part = slice(b * step, (b + 1) * step)
        onehot = jnp.where(place == spot[:, part], jnp.bfloat16(1), jnp.bfloat16(0))
        fresh_ref[:, part] = jnp.dot(
            turned_ref[...], onehot, preferred_element_type=jnp.float32
        ).astype(jnp.bfloat16)
        copy = pltpu.make_async_copy(fresh_ref.at[:, part], fresh_hbm.at[:, part], sem.at[b])
        copy.start()
        copies.append(copy)
    for copy in copies:
        copy.wait()


def cost(depth, rows, columns, *arrays):
    moved = sum(x.size * x.dtype.itemsize for x in arrays)
    return pl.CostEstimate(
        flops=2 * depth * rows * columns, transcendentals=0, bytes_accessed=moved
    )


VMEM = pl.BlockSpec(memory_space=pltpu.VMEM)
HBM = pl.BlockSpec(memory_space=pltpu.HBM)


def pack(owner, row, grad, owners, cap):
    width, tokens = grad.shape
    wide = -(-(width + 2) // 128) * 128
    sent = jax.ShapeDtypeStruct((owners * cap, wide), jnp.bfloat16)
    return pl.pallas_call(
        functools.partial(pack_kernel, owners, cap),
        out_shape=(
            sent,
            jax.ShapeDtypeStruct((1, tokens), jnp.int32),
        ),
        in_specs=[HBM, HBM, HBM],
        out_specs=(VMEM, VMEM),
        scratch_shapes=[
            pltpu.VMEM((wide, tokens), jnp.bfloat16),
            pltpu.VMEM((1, tokens), jnp.int32),
            pltpu.VMEM((1, tokens), jnp.int32),
            pltpu.SemaphoreType.DMA((3,)),
        ],
        compiler_params=pltpu.CompilerParams(vmem_limit_bytes=LIMIT),
        cost_estimate=cost(tokens, owners * cap, wide, owner, row, grad, sent),
        name="pack",
    )(*(pltpu.with_memory_space_constraint(x, pltpu.HBM) for x in (owner, row, grad)))


def update(received, accum, table):
    slots, wide = received.shape
    width, rows = table.shape
    tile = in_tile(rows)
    return pl.pallas_call(
        update_kernel,
        out_shape=(
            jax.ShapeDtypeStruct((width, rows), jnp.float32),
            jax.ShapeDtypeStruct((width, tile), jnp.float32),
            jax.ShapeDtypeStruct((1, rows), jnp.float32),
            jax.ShapeDtypeStruct((slots // 2, 2 * width), jnp.bfloat16),
        ),
        in_specs=[VMEM, VMEM, VMEM],
        out_specs=(HBM, VMEM, HBM, VMEM),
        scratch_shapes=[
            pltpu.VMEM((wide, slots), jnp.bfloat16),
            pltpu.VMEM((width, rows), jnp.bfloat16),
            pltpu.VMEM((1, rows), jnp.float32),
            pltpu.SemaphoreType.DMA,
            pltpu.VMEM((width, rows - tile), jnp.float32),
            pltpu.SemaphoreType.DMA((2,)),
        ],
        compiler_params=pltpu.CompilerParams(vmem_limit_bytes=LIMIT),
        cost_estimate=cost(2 * slots, rows, width, received, accum, table, table),
        name="update",
    )(received, accum, table)


def unpack(back, target, rest, table, cap):
    tokens = target.shape[1]
    width = table.shape[0]
    return pl.pallas_call(
        functools.partial(unpack_kernel, cap),
        out_shape=(
            jax.ShapeDtypeStruct((width, tokens), jnp.bfloat16),
            jax.ShapeDtypeStruct(table.shape, jnp.float32),
        ),
        in_specs=[VMEM, VMEM, VMEM, HBM],
        out_specs=(HBM, HBM),
        input_output_aliases={3: 1},
        scratch_shapes=[
            pltpu.VMEM((width, 2 * back.shape[0]), jnp.bfloat16),
            pltpu.VMEM((width, tokens), jnp.bfloat16),
            pltpu.SemaphoreType.DMA((2,)),
            pltpu.SemaphoreType.DMA((4,)),
        ],
        compiler_params=pltpu.CompilerParams(vmem_limit_bytes=LIMIT),
        cost_estimate=cost(2 * back.shape[0], width, tokens, back, table),
        name="unpack",
    )(back, target, rest, table)


def exchange(value, devices):
    blocks = value.reshape(devices, -1, value.shape[1])
    blocks = lax.all_to_all(blocks, AXES, split_axis=0, concat_axis=0, tiled=True)
    return blocks.reshape(value.shape)


def body(token_grad, token_owner, token_row, table, accum):
    devices = lax.axis_size(AXES)
    tokens, width = token_grad.shape
    cap = 2 * tokens // devices
    send, target = pack(
        token_owner.reshape(1, tokens), token_row.reshape(1, tokens), token_grad.T, devices, cap
    )
    received = exchange(send, devices)
    early, rest, new_accum, answers = update(received, accum.reshape(1, -1), table.T)
    back = exchange(answers, devices)
    fresh, new_table = unpack(back, target, rest, early, cap)
    return (new_table.T, new_accum.reshape(-1), fresh.T)


def solution(mesh):
    split = P(AXES)
    wide = P(AXES, None)
    return jax.shard_map(
        body,
        mesh=mesh,
        in_specs=(wide, wide, split, wide, split),
        out_specs=(wide, split, wide),
        check_vma=False,
    )
```

```python
import functools

import jax
import jax.numpy as jnp
from jax import lax
from jax.experimental import pallas as pl
from jax.experimental.pallas import tpu as pltpu
from jax.sharding import PartitionSpec as P

AXES = ("gx", "gy", "gz")
RADIX = 64
ROW_LANES = 64
LIMIT = 36 << 20


def pack_kernel(
    owners, cap, owner_hbm, row_hbm, grad_hbm, send_ref, target_ref,
    ext_ref, owner_ref, row_ref, sem,
):
    width, tokens = grad_hbm.shape
    owner_load = pltpu.make_async_copy(owner_hbm, owner_ref, sem.at[0])
    row_load = pltpu.make_async_copy(row_hbm, row_ref, sem.at[1])
    load = pltpu.make_async_copy(grad_hbm, ext_ref.at[0:width, :], sem.at[2])
    owner_load.start()
    row_load.start()
    load.start()
    owner_load.wait()
    row_load.wait()
    own = owner_ref[...]
    chunk = min(256, tokens)
    first = lax.broadcasted_iota(jnp.int32, (chunk, chunk), 0)
    second = lax.broadcasted_iota(jnp.int32, (chunk, chunk), 1)
    earlier = jnp.where(first < second, 1.0, 0.0).astype(jnp.bfloat16)
    ids = lax.broadcasted_iota(jnp.int32, (owners, chunk), 0)
    seen = jnp.zeros((owners, 1), jnp.float32)
    for c in range(tokens // chunk):
        part = slice(c * chunk, (c + 1) * chunk)
        named = ids == own[:, part]
        ones = jnp.where(named, 1.0, 0.0)
        before = jnp.dot(ones.astype(jnp.bfloat16), earlier, preferred_element_type=jnp.float32)
        rank = jnp.sum(jnp.where(named, before + seen, 0.0), axis=0, keepdims=True)
        seen = seen + jnp.sum(ones, axis=1, keepdims=True)
        target_ref[:, part] = own[:, part] * cap + rank.astype(jnp.int32)
    row = row_ref[...]
    high = row // RADIX
    low = row - high * RADIX
    extra = ext_ref.shape[0] - width
    place = lax.broadcasted_iota(jnp.int32, (extra, tokens), 0)
    tail = jnp.where(place == 0, high, jnp.where(place == 1, low, 0))
    ext_ref[width:, :] = tail.astype(jnp.float32).astype(jnp.bfloat16)
    load.wait()
    slots = send_ref.shape[0]
    wide = width + 16
    step = min(512, slots)
    slot = lax.broadcasted_iota(jnp.int16, (step, tokens), 0)
    target = jnp.broadcast_to(target_ref[...], (16, tokens)).astype(jnp.int16)[0:1]
    one, zero = jnp.bfloat16(1), jnp.bfloat16(0)
    for b in range(slots // step):
        onehot = jnp.where(slot == target - jnp.int16(b * step), one, zero)
        placed = lax.dot_general(
            ext_ref[0:wide, :], onehot, (((1,), (1,)), ((), ())),
            preferred_element_type=jnp.float32,
        ).astype(jnp.bfloat16)
        send_ref[b * step : (b + 1) * step, 0:wide] = placed.T


def copies_of(source, target, sem):
    count = sem.shape[0]
    piece = source.shape[1] // count
    parts = [slice(i * piece, (i + 1) * piece) for i in range(count)]
    return [
        pltpu.make_async_copy(source.at[:, part], target.at[:, part], sem.at[i])
        for i, part in enumerate(parts)
    ]


def update_kernel(
    recv_ref, accum_ref, table_ref, new_hbm, rest_ref, grown_hbm, answer_ref,
    turned_ref, rounded_ref, grown_ref, sem, new_ref, new_sem,
):
    width, rows = table_ref.shape
    slots = recv_ref.shape[0]
    tile = in_tile(rows)
    tiles = rows // tile
    turned_ref[...] = recv_ref[...].T
    across = turned_ref[width : width + 16, :].astype(jnp.float32).astype(jnp.int32)
    row_across = across[0:1, :] * RADIX + across[1:2, :]
    row_across = jnp.broadcast_to(row_across, (16, slots)).astype(jnp.int16)[0:1]
    one, zero = jnp.bfloat16(1), jnp.bfloat16(0)

    def summed_of(j):
        place = lax.broadcasted_iota(jnp.int16, (tile, slots), 0)
        onehot = jnp.where(place == row_across - jnp.int16(j * tile), one, zero)
        return lax.dot_general(
            turned_ref[0:width, :], onehot, (((1,), (1,)), ((), ())),
            preferred_element_type=jnp.float32,
        )

    def settle(j, summed):
        part = pl.ds(j * tile, tile)
        grown = accum_ref[:, part] + jnp.sum(summed * summed, axis=0, keepdims=True) / width
        grown_ref[:, part] = grown
        scale = 0.5 / (jnp.sqrt(grown) + 1e-08)
        moved = table_ref[:, part] - summed * scale
        if j + 1 < tiles:
            new_ref[:, part] = moved
        else:
            rest_ref[...] = moved
        rounded_ref[:, part] = moved.astype(jnp.bfloat16)

    step = min(512, slots)

    def picked_of(first, last, b):
        below = lax.broadcasted_iota(jnp.int16, (last - first, step), 0)
        wanted = row_across[:, b * step : (b + 1) * step] - jnp.int16(first)
        onehot = jnp.where(below == wanted, one, zero)
        return jnp.dot(
            rounded_ref[:, first:last], onehot, preferred_element_type=jnp.float32
        )

    early = rows - tile
    ahead = summed_of(0)
    for j in range(tiles):
        summed = ahead
        if j + 1 < tiles:
            ahead = summed_of(j + 1)
        elif early:
            begun = picked_of(0, early, 0)
        settle(j, summed)
    grown_copy = pltpu.make_async_copy(grown_ref, grown_hbm, sem)
    grown_copy.start()
    copies = copies_of(new_ref, new_hbm.at[:, 0:early], new_sem)
    for copy in copies:
        copy.start()

    for b in range(slots // step):
        if b == 0 and early:
            picked = begun + picked_of(early, rows, b)
        else:
            picked = picked_of(0, rows, b)
        picked = picked.T.reshape(step // 16, 2, 8, width)
        lower = picked[:, 0].reshape(step // 2, width)
        upper = picked[:, 1].reshape(step // 2, width)
        answer_ref[b * step // 2 : (b + 1) * step // 2, :] = jnp.concatenate(
            [lower, upper], axis=1
        ).astype(jnp.bfloat16)
    grown_copy.wait()
    for copy in copies:
        copy.wait()


def in_tile(rows):
    return min(2048, rows)


def unpack_kernel(
    cap, back_ref, target_ref, rest_ref, part_hbm, fresh_hbm, table_hbm, turned_ref, fresh_ref, sem, table_sem
):
    rows, tile = table_hbm.shape[1], rest_ref.shape[1]
    copies = copies_of(rest_ref, table_hbm.at[:, rows - tile : rows], table_sem)
    for copy in copies:
        copy.start()
    width, tokens = fresh_hbm.shape
    half = back_ref.shape[0]
    target = target_ref[...]
    owner = target // cap
    rank = target - owner * cap
    side = rank // 8
    spot = side * half + owner * 8 + rank - 8 * side
    spot = jnp.broadcast_to(spot, (16, tokens)).astype(jnp.int16)[0:1]
    turned = back_ref[...].T
    turned_ref[:, 0:half] = turned[0:width]
    turned_ref[:, half:] = turned[width:]
    edges = [0, tokens // 2, 3 * tokens // 4, tokens]
    for b in range(3):
        part = slice(edges[b], edges[b + 1])
        place = lax.broadcasted_iota(jnp.int16, (2 * half, edges[b + 1] - edges[b]), 0)
        onehot = jnp.where(place == spot[:, part], jnp.bfloat16(1), jnp.bfloat16(0))
        fresh_ref[:, part] = jnp.dot(
            turned_ref[...], onehot, preferred_element_type=jnp.float32
        ).astype(jnp.bfloat16)
        copy = pltpu.make_async_copy(fresh_ref.at[:, part], fresh_hbm.at[:, part], sem.at[b])
        copy.start()
        copies.append(copy)
    for copy in copies:
        copy.wait()


def cost(depth, rows, columns, *arrays):
    moved = sum(x.size * x.dtype.itemsize for x in arrays)
    return pl.CostEstimate(
        flops=2 * depth * rows * columns, transcendentals=0, bytes_accessed=moved
    )


VMEM = pl.BlockSpec(memory_space=pltpu.VMEM)
HBM = pl.BlockSpec(memory_space=pltpu.HBM)


def pack(owner, row, grad, owners, cap):
    width, tokens = grad.shape
    wide = -(-(width + 2) // 128) * 128
    sent = jax.ShapeDtypeStruct((owners * cap, wide), jnp.bfloat16)
    return pl.pallas_call(
        functools.partial(pack_kernel, owners, cap),
        out_shape=(
            sent,
            jax.ShapeDtypeStruct((1, tokens), jnp.int32),
        ),
        in_specs=[HBM, HBM, HBM],
        out_specs=(VMEM, VMEM),
        scratch_shapes=[
            pltpu.VMEM((wide, tokens), jnp.bfloat16),
            pltpu.VMEM((1, tokens), jnp.int32),
            pltpu.VMEM((1, tokens), jnp.int32),
            pltpu.SemaphoreType.DMA((3,)),
        ],
        compiler_params=pltpu.CompilerParams(vmem_limit_bytes=LIMIT),
        cost_estimate=cost(tokens, owners * cap, wide, owner, row, grad, sent),
        name="pack",
    )(*(pltpu.with_memory_space_constraint(x, pltpu.HBM) for x in (owner, row, grad)))


def update(received, accum, table):
    slots, wide = received.shape
    width, rows = table.shape
    tile = in_tile(rows)
    return pl.pallas_call(
        update_kernel,
        out_shape=(
            jax.ShapeDtypeStruct((width, rows), jnp.float32),
            jax.ShapeDtypeStruct((width, tile), jnp.float32),
            jax.ShapeDtypeStruct((1, rows), jnp.float32),
            jax.ShapeDtypeStruct((slots // 2, 2 * width), jnp.bfloat16),
        ),
        in_specs=[VMEM, VMEM, VMEM],
        out_specs=(HBM, VMEM, HBM, VMEM),
        scratch_shapes=[
            pltpu.VMEM((wide, slots), jnp.bfloat16),
            pltpu.VMEM((width, rows), jnp.bfloat16),
            pltpu.VMEM((1, rows), jnp.float32),
            pltpu.SemaphoreType.DMA,
            pltpu.VMEM((width, rows - tile), jnp.float32),
            pltpu.SemaphoreType.DMA((2,)),
        ],
        compiler_params=pltpu.CompilerParams(vmem_limit_bytes=LIMIT),
        cost_estimate=cost(2 * slots, rows, width, received, accum, table, table),
        name="update",
    )(received, accum, table)


def unpack(back, target, rest, table, cap):
    tokens = target.shape[1]
    width = table.shape[0]
    return pl.pallas_call(
        functools.partial(unpack_kernel, cap),
        out_shape=(
            jax.ShapeDtypeStruct((width, tokens), jnp.bfloat16),
            jax.ShapeDtypeStruct(table.shape, jnp.float32),
        ),
        in_specs=[VMEM, VMEM, VMEM, HBM],
        out_specs=(HBM, HBM),
        input_output_aliases={3: 1},
        scratch_shapes=[
            pltpu.VMEM((width, 2 * back.shape[0]), jnp.bfloat16),
            pltpu.VMEM((width, tokens), jnp.bfloat16),
            pltpu.SemaphoreType.DMA((3,)),
            pltpu.SemaphoreType.DMA((4,)),
        ],
        compiler_params=pltpu.CompilerParams(vmem_limit_bytes=LIMIT),
        cost_estimate=cost(2 * back.shape[0], width, tokens, back, table),
        name="unpack",
    )(back, target, rest, table)


def exchange(value, devices):
    blocks = value.reshape(devices, -1, value.shape[1])
    blocks = lax.all_to_all(blocks, AXES, split_axis=0, concat_axis=0, tiled=True)
    return blocks.reshape(value.shape)


def body(token_grad, token_owner, token_row, table, accum):
    devices = lax.axis_size(AXES)
    tokens, width = token_grad.shape
    cap = 2 * tokens // devices
    send, target = pack(
        token_owner.reshape(1, tokens), token_row.reshape(1, tokens), token_grad.T, devices, cap
    )
    received = exchange(send, devices)
    early, rest, new_accum, answers = update(received, accum.reshape(1, -1), table.T)
    back = exchange(answers, devices)
    fresh, new_table = unpack(back, target, rest, early, cap)
    return (new_table.T, new_accum.reshape(-1), fresh.T)


def solution(mesh):
    split = P(AXES)
    wide = P(AXES, None)
    return jax.shard_map(
        body,
        mesh=mesh,
        in_specs=(wide, wide, split, wide, split),
        out_specs=(wide, split, wide),
        check_vma=False,
    )
```
